256 devices in a mesh: row: 16 (over z, y_hi), col: 16 (over x, y_lo, core).
Axes of the slice: x: 4, y: 4 (y_hi: 2, y_lo: 2; y = y_hi * 2 + y_lo), z: 8, core: 2. Of those that a mesh axis runs over, the one named last changes fastest.
Arguments:
- similarity: bfloat16 [8192, 8192], P('row', 'col'), may hold values from 0.0009 to 1
- occupancy: int32 [64, 64], P('row', 'col'), may hold values from 0 to 1, as said below
- kept_tiles: int32 [64, 64], P('row', 'col'), may hold values from 0 to 1, as said below
Outputs:
- flow: bfloat16 [8192, 8192], P('row', 'col')
The draws below stay inside these ranges and needn't reach their ends.
Inputs may be any that keep to these rules, and one draw needn't show every extreme that they name: `occupancy`: 0 or 1; every diagonal tile is 1; the share of ones varies from tile row to tile row. `kept_tiles`: 0 or 1; every diagonal tile is 1; the share of ones varies from tile row to tile row.
All inputs are finite; a program needn't handle non-finite values.
Results may differ from the reference program's by a relative error of at most 0.001.
Values may be sent and summed in bfloat16 or wider, within the bound.
No kernel may reach another device: no remote copies, remote signals or barrier semaphores. Data moves between devices by JAX's collectives and lax.ppermute only.
A program may use at most 64 MiB of HBM per device.

```python
import jax
import jax.numpy as jnp
from jax import lax

TILE = 128
NT = 64
N = 8192


def tile_draw(key, salt):
    first, second = jax.random.split(jax.random.fold_in(key, salt))
    level = jax.random.randint(first, (NT, 1), 20, 95)
    rolls = jax.random.randint(second, (NT, NT), 0, 100)
    picked = (rolls < level).astype(jnp.int32)
    diagonal = lax.broadcasted_iota(jnp.int32, (NT, NT), 0) == lax.broadcasted_iota(jnp.int32, (NT, NT), 1)
    return jnp.where(diagonal, 1, picked).astype(jnp.int32)


def draw_occupancy(key, part):
    return tile_draw(key, 11)


def draw_kept_tiles(key, part):
    return tile_draw(key, 23)


def draw_similarity(key, part):
    base_key, pick_key, value_key = jax.random.split(jax.random.fold_in(key, 37), 3)
    weak = jax.random.uniform(base_key, (N, N), jnp.float32, 0.001, 0.005)
    rolls = jax.random.uniform(pick_key, (N, N), jnp.float32, 0.0, 1.0)
    strong = jnp.exp(jax.random.uniform(value_key, (N, N), jnp.float32, jnp.log(0.1), 0.0))
    chosen = rolls < 0.06
    return jnp.where(chosen, strong, weak).astype(jnp.bfloat16)


def setup_inputs(seed: int = 0) -> dict:
    key_of = jax.random.split(jax.random.key(seed), 4)
    return {
        "similarity": draw_similarity(jax.random.fold_in(key_of[3], 71), 0),
        "occupancy": draw_occupancy(jax.random.fold_in(key_of[3], 71), 0),
        "kept_tiles": draw_kept_tiles(jax.random.fold_in(key_of[3], 71), 0),
    }


def expand_tiles(values, tile_pattern, tile_size):
    rows, cols = values.shape
    shaped = values.reshape(rows // tile_size, tile_size, cols // tile_size, tile_size)
    masked = shaped * tile_pattern.astype(values.dtype)[:, None, :, None]
    return masked.reshape(rows, cols)


def reference(similarity, occupancy, kept_tiles):
    stored = expand_tiles(similarity, occupancy, TILE)
    wide = stored.astype(jnp.float32)
    expanded = jnp.dot(wide, wide, preferred_element_type=jnp.float32)
    inflated = expand_tiles(expanded * expanded, kept_tiles, TILE)
    column_total = jnp.sum(inflated, axis=0)
    return (N * inflated / column_total[None, :]).astype(jnp.bfloat16)
```

```python
import jax
import jax.numpy as jnp
from jax import lax
from jax.sharding import Mesh, PartitionSpec as P

TILE = 128
AXES = ("z", "yh", "x", "yl", "core")
SIZES = (8, 2, 4, 2, 2)
GROUPS = 2


def pairs(move):
    found = []
    nz, nyh, nx, nyl, nc = SIZES

    def flat(z, yh, x, yl, c):
        return (((z % nz * nyh + yh) * nx + x % nx) * nyl + yl) * nc + c

    for z in range(nz):
        for yh in range(nyh):
            for x in range(nx):
                for yl in range(nyl):
                    for c in range(nc):
                        target = move(z, yh, x, yl, c)
                        if target is not None:
                            found.append((flat(z, yh, x, yl, c), flat(*target)))
    return found


Z_UP = pairs(lambda z, yh, x, yl, c: (z + 1, yh, x, yl, c))
Z_DOWN = pairs(lambda z, yh, x, yl, c: (z - 1, yh, x, yl, c))
X_UP = pairs(lambda z, yh, x, yl, c: (z, yh, x + 1, yl, c))
X_DOWN = pairs(lambda z, yh, x, yl, c: (z, yh, x - 1, yl, c))
YH_SWAP = pairs(lambda z, yh, x, yl, c: (z, 1 - yh, x, yl, c))
CORE_SWAP = pairs(lambda z, yh, x, yl, c: (z, yh, x, yl, 1 - c))
AWAY_FAR = pairs(lambda z, yh, x, yl, c: (z, c, x, yl, c) if c != yh else None)
AWAY_NEAR = pairs(lambda z, yh, x, yl, c: (z, c, x, 1 - yl, 1 - c) if c != yh else None)
HOME_NEAR = pairs(lambda z, yh, x, yl, c: (z, yh, x, 1 - yl, 1 - c) if c == yh else None)


def move(value, permutation):
    return lax.ppermute(value, AXES, permutation)


def expand_tiles(values, tile_pattern, tile_size):
    rows, cols = values.shape
    shaped = values.reshape(rows // tile_size, tile_size, cols // tile_size, tile_size)
    masked = shaped * tile_pattern.astype(values.dtype)[:, None, :, None]
    return masked.reshape(rows, cols)


def gather_left(block, first_up):
    up = move(block, X_UP)
    down = move(block, X_DOWN)
    across = move(up, X_UP) if first_up else move(down, X_DOWN)
    mine = jnp.stack([block, down, across, up])
    return jnp.concatenate([mine, move(mine, CORE_SWAP)])


def body(similarity, occupancy, kept_tiles):
    rows, cols = similarity.shape
    order = rows * 16
    z, yh, x, yl, core = (lax.axis_index(a) for a in AXES)
    home = core == yh
    stored = expand_tiles(similarity, occupancy, TILE)
    width = cols // GROUPS

    right = []
    for g in range(GROUPS):
        block = stored[:, g * width : (g + 1) * width]
        found = {0: block}
        up = down = block
        for step in range(1, 4):
            up, down = move(up, Z_UP), move(down, Z_DOWN)
            found[8 - step], found[step] = up, down
        found[4] = move(up, Z_UP) if g % 2 == 0 else move(down, Z_DOWN)
        right.append(found)

    far, near = move(stored, AWAY_FAR), move(stored, AWAY_NEAR)
    left_sent = gather_left(jnp.where(home, far, near), True)
    left_kept = gather_left(jnp.where(home, stored, move(stored, HOME_NEAR)), False)

    mine_yl = jnp.where(home, yl, 1 - yl)

    def partial(left, found):
        total = None
        for d in (0, 1, 7, 2, 6, 3, 5, 4):
            k = (z + d) % 8
            slot = (k // 2 - x) % 4 + jnp.where(k % 2 == mine_yl, 0, 4)
            a = lax.dynamic_index_in_dim(left, slot, 0, keepdims=False)
            term = jnp.dot(a, found[d], preferred_element_type=jnp.float32)
            total = term if total is None else total + term
        return total

    keep_mask = expand_tiles(jnp.ones((rows, cols), jnp.float32), kept_tiles, TILE)
    inflated, sums = [], []
    for g in range(GROUPS):
        received = move(partial(left_sent, right[g]), YH_SWAP)
        expanded = partial(left_kept, right[g]) + received
        value = expanded * expanded * keep_mask[:, g * width : (g + 1) * width]
        inflated.append(value)
        sums.append(jnp.sum(value, axis=0))
    mine = jnp.concatenate(sums)
    spread = jnp.broadcast_to(mine[None, None, :], (16, 1, cols))
    column_total = lax.all_to_all(spread, ("z", "yh"), 0, 0, tiled=True).sum(axis=(0, 1))
    results = []
    for g in range(GROUPS):
        total = column_total[g * width : (g + 1) * width]
        results.append((order * inflated[g] / total[None, :]).astype(jnp.bfloat16))
    return jnp.concatenate(results, axis=1)


def solution(mesh):
    split = Mesh(mesh.devices.reshape(SIZES), AXES)
    spec = P(("z", "yh"), ("x", "yl", "core"))
    return jax.shard_map(body, mesh=split, in_specs=(spec,) * 3, out_specs=spec, check_vma=False)
```
